32 devices in a mesh: groups: 2 (over y), ctx: 4 (over z), head: 2 (over x), dp: 2 (over core).
Axes of the slice: x: 2, y: 2, z: 4, core: 2. Of those that a mesh axis runs over, the one named last changes fastest.
Arguments:
- query_input: bfloat16 [4, 512, 16, 128], P(('groups', 'dp'), 'ctx', 'head'), parts along dimension 0, may hold values from -6 to 6
- key_input: bfloat16 [4, 512, 3, 16, 128], P(('groups', 'dp'), 'ctx', None, 'head'), parts along dimension 0, may hold values from -6 to 6
- value_input: bfloat16 [4, 512, 3, 16, 128], P(('groups', 'dp'), 'ctx', None, 'head'), parts along dimension 0, may hold values from -6 to 6
- beta_logit: float32 [4, 16, 3, 512], P(('groups', 'dp'), 'head', None, 'ctx'), parts along dimension 0, may hold values from -6 to 6
- gate_logit: float32 [4, 16, 512], P(('groups', 'dp'), 'head', 'ctx'), parts along dimension 0, may hold values from -6 to 1536
- decay_rate: float32 [16], P('head'), may hold values from 0.00048828125 to 0.05
- doc_ids: int32 [4, 8], P(('groups', 'dp')), parts along dimension 0, may hold values from 0 to 1, never falling along the last dimension, each value on 1 to 7 neighbouring positions
- out_weight: bfloat16 [2048, 2048], P('head'), may hold values from -0.125 to 0.125
- out_cotangent: bfloat16 [4, 512, 2048], P(('groups', 'dp'), 'ctx'), parts along dimension 0, may hold values from -6 to 6
Outputs:
- mixed: bfloat16 [4, 512, 2048], P(('groups', 'dp'), 'ctx', 'head'), parts along dimension 0
- query_grad: bfloat16 [4, 512, 16, 128], P(('groups', 'dp'), 'ctx', 'head'), parts along dimension 0
- key_grad: bfloat16 [4, 512, 3, 16, 128], P(('groups', 'dp'), 'ctx', None, 'head'), parts along dimension 0
- value_grad: bfloat16 [4, 512, 3, 16, 128], P(('groups', 'dp'), 'ctx', None, 'head'), parts along dimension 0
- beta_grad: float32 [4, 16, 3, 512], P(('groups', 'dp'), 'head', None, 'ctx'), parts along dimension 0
- gate_grad: float32 [4, 16, 512], P(('groups', 'dp'), 'head', 'ctx'), parts along dimension 0
- weight_grad: float32 [4096, 2048], P(('groups', 'ctx'), 'head'), parts along dimension 0
- rate_grad: float32 [32], P(('groups', 'head')), parts along dimension 0
The draws below stay inside these ranges and needn't reach their ends.
There are 2 independent parts, one for each index of `groups`. The reference program is written for one: setup_inputs(seed, part) draws one part's arguments, and reference() takes and returns one part's arrays. A program takes and returns all parts, laid end to end along the dimension named above; an argument that names none is the same for every part. Nothing has to cross between parts.
Inputs may be any that keep to these rules, and one draw needn't show every extreme that they name: `doc_ids`: in each sequence the numbers never fall along the stretches, every number of 0 to 1 appears, each covers 1 to 7 stretches.
All inputs are finite; a program needn't handle non-finite values.
Results may differ from the reference program's by a relative error of at most 0.0051.
Values sent between devices are 32-bit elements; how exact they have to be, the bound alone decides.
A program may use at most 192 MiB of HBM per device.

```python
import math
import jax
import jax.numpy as jnp
import numpy as np
from jax import lax

CH = 64
NF = 3
D = 2048
H = 16
DK = 128
DV = 128
BATCH_DOCUMENTS = 2
CONTEXT_LENGTH = 512
NCHUNK = 8
DOCS = 2
MOSTC = 7


def draw_gate_logit(key, part):
    base_key, layout_seed, size_key = jax.random.split(jax.random.fold_in(key, 11), 3)
    baseline = jnp.clip(jax.random.normal(base_key, (BATCH_DOCUMENTS, H, CONTEXT_LENGTH), jnp.float32), -6.0, 6.0)
    segment_clusters = jax.random.randint(layout_seed, (BATCH_DOCUMENTS, 4, 1), 0, CONTEXT_LENGTH)
    flagged_lines = jnp.any(jnp.arange(CONTEXT_LENGTH)[None, None, :] == segment_clusters, axis=1)
    heights = jax.random.uniform(size_key, (BATCH_DOCUMENTS, 1, CONTEXT_LENGTH), jnp.float32, 1.0, 2.8) * CONTEXT_LENGTH
    return jnp.where(flagged_lines[:, None, :], heights, baseline)


def draw_decay_rate(key, part):
    lowest = 0.25 / CONTEXT_LENGTH
    highest_level = 0.05
    fraction = jax.random.uniform(jax.random.fold_in(key, 23), (H,), jnp.float32)
    return jnp.exp(jnp.log(lowest) + fraction * (jnp.log(highest_level) - jnp.log(lowest)))


def raised(result, key, source, target, blocks, factor):
    def block_of(position):
        return (jnp.arange(result.shape[position]) // (result.shape[position] // blocks)).reshape((-1,) + (1,) * (result.ndim - 1 - position))

    near = jax.random.permutation(key, blocks)[block_of(target)]
    second = (block_of(target) + blocks // 2) % blocks
    return jnp.where((block_of(source) == near) | (block_of(source) == second), factor * result, result)


def block_scale(own_key, dims, cuts, low, largest):
    loudness, own = 1.0, jax.random.fold_in(own_key, 6)
    for position, parts in cuts:
        steps = jnp.exp(jax.random.uniform(jax.random.fold_in(own, position), (parts,), jnp.float32, low / len(cuts), largest / len(cuts)))
        loudness = loudness * jnp.repeat(steps, dims[position] // parts).reshape([-1 if axis == position else 1 for axis in range(len(dims))])
    return loudness


def profile(number_of, total, limit, slope):
    weights = [(1 << 20) // math.isqrt(standing ** slope) + 1 for standing in range(2, number_of + 1)]
    rest, counts = total - limit - (number_of - 1), [1] * (number_of - 1)
    while rest > 0:
        movable = [i for i in range(number_of - 1) if counts[i] < limit]
        whole, remaining = sum([weights[i] for i in movable]), rest
        for i in movable:
            addition = min(limit - counts[i], max(1, remaining * weights[i] // whole), rest)
            counts[i] = counts[i] + addition
            rest = rest - addition
    return np.array([limit] + counts)


def ragged_sizes(key, count, total, most, lean):
    if count == 2:
        one = jax.random.randint(key, (), max(1, total - most), min(most, total - 1) + 1)
        return jnp.stack([one, total - one])
    lengths = jnp.asarray(profile(count, total, most, lean), jnp.int32)
    pairs = (count - 1) // 2
    source_of, sink = lengths[1:1 + 2 * pairs:2], lengths[2:2 + 2 * pairs:2]
    margin = jnp.minimum(source_of - 1, most - sink)
    moved = jax.random.randint(jax.random.fold_in(key, 1), (pairs,), 0, 1 << 20) % (margin + 1)
    lengths = lengths.at[1:1 + 2 * pairs:2].set(source_of - moved).at[2:2 + 2 * pairs:2].set(sink + moved)
    return lengths[jax.random.permutation(jax.random.fold_in(key, 2), count)]


def bell_draw(stream_key, shape, scale, reach, cuts=(), kind=jnp.bfloat16):
    drawn = scale * jax.random.normal(stream_key, shape, jnp.float32)
    if cuts:
        drawn = drawn * block_scale(stream_key, shape, cuts, -0.22, 0.18)
    return jnp.clip(drawn, -reach, reach).astype(kind)


def heavy_noise(stream_key, dims, scale, bound, cuts, heavy, kind=jnp.bfloat16):
    values = scale * jax.random.normal(stream_key, dims, jnp.float32)
    if cuts:
        values = values * block_scale(stream_key, dims, cuts, -0.22, 0.18)
    return jnp.clip(raised(values, jax.random.fold_in(stream_key, 3), *heavy), -bound, bound).astype(kind)


def setup_inputs(seed: int = 0, part: int = 0) -> dict:
    streams_of = jax.random.split(jax.random.key(seed), 10)
    part_splits = jax.random.split(jax.random.fold_in(streams_of[9], part), 10)
    return {
        "query_input": bell_draw(part_splits[0], (BATCH_DOCUMENTS, CONTEXT_LENGTH, H, DK), 1.0, 6.0, ((0, 2), (1, 4), (2, 2))),
        "key_input": bell_draw(part_splits[1], (BATCH_DOCUMENTS, CONTEXT_LENGTH, NF, H, DK), 1.0, 6.0, ((0, 2), (1, 4), (3, 2))),
        "value_input": bell_draw(part_splits[2], (BATCH_DOCUMENTS, CONTEXT_LENGTH, NF, H, DV), 1.0, 6.0, ((0, 2), (1, 4), (3, 2))),
        "beta_logit": bell_draw(part_splits[3], (BATCH_DOCUMENTS, H, NF, CONTEXT_LENGTH), 1.5, 6.0, ((0, 2), (1, 2), (3, 4)), jnp.float32),
        "gate_logit": draw_gate_logit(jax.random.fold_in(jax.random.fold_in(streams_of[9], part), 71), part),
        "decay_rate": draw_decay_rate(jax.random.fold_in(streams_of[9], 71), part),
        "doc_ids": jax.vmap(lambda own: jnp.searchsorted(jnp.cumsum(ragged_sizes(own, DOCS, NCHUNK, MOSTC, 1)), jnp.arange(NCHUNK), side="right"))(jax.random.split(part_splits[6], BATCH_DOCUMENTS)).reshape((BATCH_DOCUMENTS, NCHUNK)).astype(jnp.int32),
        "out_weight": bell_draw(streams_of[7], (H * DK, D), (H * DV) ** -0.5, 0.125, ((0, 2),)),
        "out_cotangent": heavy_noise(part_splits[8], (BATCH_DOCUMENTS, CONTEXT_LENGTH, D), 1.0, 6.0, ((0, 2), (1, 4)), (1, 2, 4, 2.0)),
    }


def prepare(query_input, key_input, value_input, beta_logit, gate_logit, decay_rate):
    seq_count, length, head_count, key_width = query_input.shape
    value_width = value_input.shape[-1]
    batch = seq_count * head_count
    blocks = length // CH
    span = CH * NF
    query = (query_input * key_width ** (-0.5)).transpose(0, 2, 1, 3).reshape(batch, blocks, CH, key_width)
    squares = lax.optimization_barrier(jnp.sum(key_input * key_input, axis=-1, keepdims=True))
    keys = (key_input * lax.rsqrt(squares + 1e-06)).transpose(0, 3, 1, 2, 4).reshape(batch, blocks, span, key_width)
    values = value_input.transpose(0, 3, 1, 2, 4).reshape(batch, blocks, span, value_width)
    betas = (2.0 * jax.nn.sigmoid(beta_logit)).transpose(0, 1, 3, 2).reshape(batch, blocks, span)
    log_decay = -decay_rate[None, :, None] * jax.nn.softplus(gate_logit)
    spread = jnp.concatenate([log_decay[..., None], jnp.zeros(log_decay.shape + (NF - 1,), log_decay.dtype)], axis=-1)
    cumulative = jnp.cumsum(spread.reshape(batch, blocks, span), axis=-1)
    return tuple((jnp.moveaxis(piece, 1, 0) for piece in (query, keys, values, betas, cumulative)))

def stretch_step(carry_state, pieces):
    query_block, key_block, value_block, beta_block, cumul_block, retain_block = pieces
    highest_level = lax.Precision.HIGHEST
    value_width = value_block.shape[-1]
    total_width = carry_state.shape[-1]
    span = key_block.shape[1]
    entry = carry_state * retain_block[:, None, None]
    token_indices = jnp.arange(span)
    strict = token_indices[:, None] > token_indices[None, :]
    gap = cumul_block[:, :, None] - cumul_block[:, None, :]
    decay_pairs = jnp.exp(jnp.where(strict, gap, 0.0)) * strict
    key_gram = jnp.einsum('nid,njd->nij', key_block, key_block, precision=highest_level)
    lower_factor = jnp.eye(span, dtype=key_gram.dtype) + beta_block[:, :, None] * decay_pairs * key_gram
    growth = jnp.exp(cumul_block)
    right_side = jnp.concatenate([value_block, growth[..., None] * key_block], axis=-1) * beta_block[..., None]
    solved = jax.scipy.linalg.solve_triangular(lower_factor, right_side, lower=True, unit_diagonal=True)
    updates = jnp.pad(solved[..., :value_width], ((0, 0), (0, 0), (0, total_width - value_width)))
    correction = updates - jnp.einsum('nmk,nke->nme', solved[..., value_width:], entry, precision=highest_level)
    read_index = token_indices[NF - 1::NF]
    read_cumul = cumul_block[:, NF - 1::NF]
    visible = token_indices[None, :] <= read_index[:, None]
    read_gap = read_cumul[:, :, None] - cumul_block[:, None, :]
    read_decay = jnp.exp(jnp.where(visible, read_gap, 0.0)) * visible
    query_key = jnp.einsum('ntd,njd->ntj', query_block, key_block, precision=highest_level)
    outputs = jnp.exp(read_cumul)[..., None] * jnp.einsum('ntd,nde->nte', query_block, entry, precision=highest_level)
    outputs = outputs + jnp.einsum('ntj,nje->nte', query_key * read_decay, correction, precision=highest_level)
    last_cumul = cumul_block[:, -1]
    scaled_keys = jnp.exp(last_cumul[:, None] - cumul_block)[..., None] * key_block
    advanced = jnp.exp(last_cumul)[:, None, None] * entry + jnp.einsum('njd,nje->nde', scaled_keys, correction, precision=highest_level)
    return (advanced, outputs)

def reference(query_input, key_input, value_input, beta_logit, gate_logit, decay_rate, doc_ids, out_weight, out_cotangent):
    seq_count, length, head_count, key_width = query_input.shape
    value_width = value_input.shape[-1]
    batch = seq_count * head_count
    previous = jnp.concatenate([jnp.full((seq_count, 1), -1, jnp.int32), doc_ids[:, :-1].astype(jnp.int32)], axis=1)
    retain = jnp.repeat((doc_ids.astype(jnp.int32) == previous).astype(jnp.float32), head_count, axis=0)

    def forward(query, keys, values, betas, gates, rates):
        pieces = prepare(query, keys, values, betas, gates, rates) + (jnp.moveaxis(retain, 1, 0),)
        anchor = jnp.zeros((batch, key_width, value_width), jnp.float32)
        closing, outputs = lax.scan(jax.checkpoint(stretch_step), anchor, pieces)
        return jnp.moveaxis(outputs, 0, 1).reshape(batch, length, value_width)
    core_state, pullback = jax.vjp(forward, query_input.astype(jnp.float32), key_input.astype(jnp.float32), value_input.astype(jnp.float32), beta_logit.astype(jnp.float32), gate_logit.astype(jnp.float32), decay_rate.astype(jnp.float32))
    core_rows = core_state.reshape(seq_count, head_count, length, value_width).transpose(0, 2, 1, 3)
    core_rows = core_rows.reshape(seq_count * length, head_count * value_width).astype(jnp.bfloat16)
    mixed = jnp.dot(core_rows.astype(jnp.float32), out_weight.astype(jnp.float32), preferred_element_type=jnp.float32).astype(jnp.bfloat16)
    mixed = mixed.reshape(seq_count, length, -1)
    cot_rows = out_cotangent.reshape(seq_count * length, -1)
    core_state_grad = jnp.dot(cot_rows.astype(jnp.float32), out_weight.T.astype(jnp.float32), preferred_element_type=jnp.float32)
    core_state_grad = core_state_grad.reshape(seq_count, length, head_count, value_width).transpose(0, 2, 1, 3).reshape(batch, length, value_width)
    gradients = pullback(core_state_grad)
    weight_grad = jnp.dot(cot_rows.T.astype(jnp.float32), core_rows.astype(jnp.float32), preferred_element_type=jnp.float32)
    return (mixed, gradients[0].astype(jnp.bfloat16), gradients[1].astype(jnp.bfloat16), gradients[2].astype(jnp.bfloat16), gradients[3], gradients[4], weight_grad, gradients[5])
```

```python
import functools

import jax
import jax.numpy as jnp
from jax import lax
from jax.experimental import pallas as pl
from jax.experimental.pallas import tpu as pltpu
from jax.sharding import PartitionSpec as P

CH = 64
NF = 3
SPAN = CH * NF
F32 = jnp.float32
BF16 = jnp.bfloat16


def mm(a, b, ta=False, tb=False, passes=1):
    dims = (((0 if ta else 1,), (1 if tb else 0,)), ((), ()))

    def one(x, y):
        return lax.dot_general(x, y, dims, preferred_element_type=F32)

    a_high, b_high = a.astype(BF16), b.astype(BF16)
    result = one(a_high, b_high)
    if passes == 3:
        a_low = (a - a_high.astype(F32)).astype(BF16)
        b_low = (b - b_high.astype(F32)).astype(BF16)
        result = result + one(a_high, b_low) + one(a_low, b_high)
    return result


def order_masks():
    row = lax.broadcasted_iota(jnp.int32, (SPAN, SPAN), 0)
    column = lax.broadcasted_iota(jnp.int32, (SPAN, SPAN), 1)
    row_time = (row % CH) * NF + row // CH
    column_time = (column % CH) * NF + column // CH
    return row_time > column_time, row_time ^ column_time


def load_stretch(s, q_ref, k_refs, v_refs, cols_ref, rows_ref):
    at = slice(s * CH, (s + 1) * CH)
    q = q_ref[at, :].astype(F32) * (q_ref.shape[-1] ** (-0.5))
    raw = jnp.concatenate([ref[at, :] for ref in k_refs], axis=0).astype(F32)
    v = jnp.concatenate([ref[at, :] for ref in v_refs], axis=0).astype(F32)
    inverse_norm = lax.rsqrt(jnp.sum(raw * raw, axis=1, keepdims=True) + 1e-06)
    k = raw * inverse_norm
    cols = cols_ref[0, at, :]
    beta = jnp.concatenate([cols[:, f : f + 1] for f in range(NF)], axis=0)
    token_cumul = cols[:, 3:4]
    token_last = cols[CH - 1 : CH, 3:4]
    cumul_row = rows_ref[0, 0:1, at]
    i = lax.broadcasted_iota(jnp.int32, (CH, CH), 0)
    j = lax.broadcasted_iota(jnp.int32, (CH, CH), 1)
    decay = jnp.where(i >= j, jnp.exp(jnp.where(i >= j, token_cumul - cumul_row, 0.0)), 0.0)
    read_decay = jnp.concatenate([decay] * NF, axis=1)
    growth = jnp.exp(token_cumul)
    tail = jnp.exp(token_last - token_cumul)
    return dict(
        q=q,
        k=k,
        v=v,
        inverse_norm=inverse_norm,
        beta=beta,
        read_decay=read_decay,
        pair_decay=jnp.concatenate([read_decay] * NF, axis=0),
        read_growth=growth,
        growth=jnp.concatenate([growth] * NF, axis=0),
        tail=jnp.concatenate([tail] * NF, axis=0),
        last=jnp.exp(token_last),
    )


def maps_kernel(
    passes, retain_ref, q_ref, k0, k1, k2, v0, v1, v2, cols_ref, rows_ref, grad_ref,
    inverse_ref, map_ref, offset_ref, pull_ref, total_map_ref, total_offset_ref, total_pull_ref,
):
    strict, differing = order_masks()
    width = q_ref.shape[-1]
    count = q_ref.shape[0] // CH
    diagonal = (
        lax.broadcasted_iota(jnp.int32, (width, width), 0)
        == lax.broadcasted_iota(jnp.int32, (width, width), 1)
    )
    parts = [load_stretch(s, q_ref, (k0, k1, k2), (v0, v1, v2), cols_ref, rows_ref) for s in range(count)]
    lowers, inverses = [], []
    for part in parts:
        gram = mm(part["k"], part["k"], tb=True, passes=passes)
        lower = jnp.where(strict, part["beta"] * part["pair_decay"] * gram, 0.0)
        lowers.append(lower)
        inverses.append(
            jnp.where(differing == 0, 1.0, 0.0) - jnp.where(differing == 1, lower, 0.0)
        )
    for level in range(1, (SPAN - 1).bit_length()):
        here = (differing >> level) == 1
        halves = [mm(jnp.where(here, low, 0.0), inv, passes=passes) for low, inv in zip(lowers, inverses)]
        inverses = [inv - mm(inv, half, passes=passes) for inv, half in zip(inverses, halves)]
    maps, offsets, pulls = [], [], []
    for s, (part, inverse) in enumerate(zip(parts, inverses)):
        inverse_ref[0, s] = inverse
        right = part["beta"] * jnp.concatenate([part["v"], part["growth"] * part["k"]], axis=1)
        solved = mm(inverse, right, passes=passes)
        moved = mm(part["tail"] * part["k"], solved, ta=True, passes=passes)
        offsets.append(moved[:, :width])
        maps.append(jnp.where(diagonal, part["last"], 0.0) - moved[:, width:])
        reads = mm(part["q"], part["k"], tb=True, passes=passes) * part["read_decay"]
        route = part["read_growth"] * part["q"] - mm(reads, solved[:, width:], passes=passes)
        pulls.append(mm(route, grad_ref[s * CH : (s + 1) * CH, :], ta=True, passes=passes))
        map_ref[0, s] = maps[-1]
        offset_ref[0, s] = offsets[-1]
        pull_ref[0, s] = pulls[-1]
    total_map, total_offset = retain_ref[0] * maps[0], offsets[0]
    for s in range(1, count):
        kept = retain_ref[s] * maps[s]
        total_map = mm(kept, total_map, passes=3)
        total_offset = mm(kept, total_offset, passes=3) + offsets[s]
    total_pull = retain_ref[count - 1] * pulls[-1]
    for s in range(count - 2, -1, -1):
        total_pull = retain_ref[s] * (pulls[s] + mm(maps[s], total_pull, ta=True, passes=3))
    total_map_ref[0] = total_map
    total_offset_ref[0] = total_offset
    total_pull_ref[0] = total_pull


def results_kernel(
    passes, retain_ref, q_ref, k0, k1, k2, v0, v1, v2, cols_ref, rows_ref, grad_ref,
    inverse_ref, map_ref, offset_ref, pull_ref, enter_ref, leave_ref,
    core_ref, dq_ref, dk0, dk1, dk2, dv0, dv1, dv2, col_out_ref, row_out_ref,
):
    strict, _ = order_masks()
    width = q_ref.shape[-1]
    count = q_ref.shape[0] // CH
    entries = [retain_ref[0] * enter_ref[0]]
    for s in range(1, count):
        entries.append(
            retain_ref[s] * (mm(map_ref[0, s - 1], entries[-1], passes=passes) + offset_ref[0, s - 1])
        )
    exits = [leave_ref[0]]
    for s in range(count - 1, 0, -1):
        exits.insert(
            0, retain_ref[s] * (mm(map_ref[0, s], exits[0], ta=True, passes=passes) + pull_ref[0, s])
        )
    mul = functools.partial(mm, passes=passes)
    for s in range(count):
        at = slice(s * CH, (s + 1) * CH)
        part = load_stretch(s, q_ref, (k0, k1, k2), (v0, v1, v2), cols_ref, rows_ref)
        q, k, beta, growth, tail = part["q"], part["k"], part["beta"], part["growth"], part["tail"]
        entry, leaving, grad = entries[s], exits[s], grad_ref[at, :]
        inverse = inverse_ref[0, s]
        gram = mul(k, k, tb=True)
        pair_decay = jnp.where(strict, part["pair_decay"], 0.0)
        on_entry = mul(jnp.concatenate([k, q], axis=0), entry)
        key_entry, query_entry = on_entry[:SPAN], on_entry[SPAN:]
        rest = part["v"] - growth * key_entry
        correction = mul(inverse, beta * rest)
        reads = mul(q, k, tb=True) * part["read_decay"]
        core_ref[at, :] = (part["read_growth"] * query_entry + mul(reads, correction)).astype(BF16)
        correction_grad = mul(reads, grad, ta=True) + tail * mul(k, leaving)
        right_grad = mul(inverse, correction_grad, ta=True)
        rest_grad = beta * right_grad
        outer = mul(jnp.concatenate([right_grad, grad], axis=0), correction, tb=True)
        scaled = -outer[:SPAN] * pair_decay
        reads_grad = outer[SPAN:]
        paired = scaled * gram
        paired_rows = jnp.sum(paired, axis=1, keepdims=True)
        beta_grad = jnp.sum(right_grad * rest, axis=1, keepdims=True) + paired_rows
        gram_grad = beta * scaled
        score_grad = reads_grad * part["read_decay"]
        read_pairs = reads_grad * reads
        back = mul(
            jnp.concatenate([-growth * rest_grad, part["read_growth"] * grad], axis=0), entry, tb=True
        )
        tail_grad = tail * mul(correction, leaving, tb=True)
        direct = mul(jnp.concatenate([gram_grad, score_grad], axis=0), k)
        query_grad = back[SPAN:] + direct[SPAN:]
        key_grad = (
            back[:SPAN] + direct[:SPAN] + tail_grad
            + mul(jnp.concatenate([gram_grad, score_grad], axis=0), jnp.concatenate([k, q], axis=0), ta=True)
        )
        tail_sums = jnp.sum(tail_grad * k, axis=1, keepdims=True)
        factor_cumul = (
            beta * paired_rows
            - growth * jnp.sum(rest_grad * key_entry, axis=1, keepdims=True)
            - tail_sums
        )
        token_cumul = (
            jnp.sum(read_pairs, axis=1, keepdims=True)
            + part["read_growth"] * jnp.sum(grad * query_entry, axis=1, keepdims=True)
        )
        for f in range(NF):
            token_cumul = token_cumul + factor_cumul[f * CH : (f + 1) * CH]
        last_grad = jnp.sum(tail_sums, axis=0, keepdims=True) + part["last"] * jnp.sum(
            jnp.sum(entry * leaving, axis=1, keepdims=True), axis=0, keepdims=True
        )
        token = lax.broadcasted_iota(jnp.int32, (CH, 1), 0)
        token_cumul = token_cumul + jnp.where(token == CH - 1, last_grad, 0.0)
        columns = jnp.sum(beta * paired, axis=0, keepdims=True) + jnp.sum(
            read_pairs, axis=0, keepdims=True
        )
        column_sums = columns[:, :CH]
        for f in range(1, NF):
            column_sums = column_sums + columns[:, f * CH : (f + 1) * CH]
        key_grad = part["inverse_norm"] * (
            key_grad - k * jnp.sum(k * key_grad, axis=1, keepdims=True)
        )
        dq_ref[at, :] = (query_grad * (width ** (-0.5))).astype(BF16)
        for f, (dk_ref, dv_ref) in enumerate(((dk0, dv0), (dk1, dv1), (dk2, dv2))):
            dk_ref[at, :] = key_grad[f * CH : (f + 1) * CH].astype(BF16)
            dv_ref[at, :] = rest_grad[f * CH : (f + 1) * CH].astype(BF16)
        col_out_ref[0, at, :] = jnp.concatenate(
            [beta_grad[f * CH : (f + 1) * CH] for f in range(NF)]
            + [token_cumul, jnp.zeros((CH, 4), F32)],
            axis=1,
        )
        row_out_ref[0, :, at] = jnp.broadcast_to(-column_sums, (8, CH))


def shifted(value, axis, steps):
    count = lax.axis_size(axis)
    first, last = (max(0, -steps), min(count, count - steps))
    return lax.ppermute(value, axis, [(source, source + steps) for source in range(first, last)])


def chain(total_map, total_offset, total_pull):
    turns = lax.axis_size("ctx") - 1
    high = lax.Precision.HIGHEST
    enter = jnp.zeros_like(total_offset)
    leave = jnp.zeros_like(total_pull)
    for _ in range(turns):
        enter = shifted(
            jnp.einsum("swa,sag->swg", total_map, enter, precision=high) + total_offset, "ctx", 1
        )
        leave = shifted(
            jnp.einsum("saw,sag->swg", total_map, leave, precision=high) + total_pull, "ctx", -1
        )
    return enter, leave


def on_device(
    query_input, key_input, value_input, beta_logit, gate_logit, decay_rate,
    doc_ids, out_weight, out_cotangent,
):
    high = lax.Precision.HIGHEST
    _, length, heads, width = query_input.shape
    model_width = out_cotangent.shape[-1]
    blocks = length // CH
    padded = jnp.concatenate([jnp.full((1, 1), -1, jnp.int32), doc_ids], axis=1)
    window = lax.dynamic_slice_in_dim(padded, lax.axis_index("ctx") * blocks, blocks + 1, 1)
    retain = (window[0, 1:] == window[0, :-1]).astype(F32)

    queries = query_input.reshape(length, heads * width)
    keys = key_input.reshape(length, NF * heads * width)
    values = value_input.reshape(length, NF * heads * width)
    sigmoid = jax.nn.sigmoid(beta_logit[0])
    betas = 2.0 * sigmoid
    soft = jax.nn.softplus(gate_logit[0])
    log_decay = (-decay_rate[:, None] * soft).reshape(heads, blocks, CH)
    ordered = (jnp.arange(CH)[:, None] <= jnp.arange(CH)[None, :]).astype(F32)
    cumulative = jnp.dot(log_decay, ordered, precision=high).reshape(heads, 1, length)
    rows = jnp.broadcast_to(cumulative, (heads, 8, length))
    cols = jnp.concatenate(
        [betas, cumulative, jnp.zeros((heads, 4, length), F32)], axis=1
    ).transpose(0, 2, 1)

    cot_rows = out_cotangent.reshape(length, model_width)
    core_grad = lax.dot_general(
        cot_rows, out_weight, (((1,), (1,)), ((), ())), preferred_element_type=F32
    )

    def lane_block(f):
        return pl.BlockSpec((length, width), lambda h: (0, f * heads + h))

    def whole(*shape):
        return pl.BlockSpec((1,) + shape, lambda h: (h,) + (0,) * len(shape))

    state = (width, width)
    common_specs = (
        [pl.BlockSpec(memory_space=pltpu.SMEM), lane_block(0)]
        + [lane_block(f) for f in range(NF)] * 2
        + [whole(length, 8), whole(8, length), lane_block(0)]
    )
    common = (retain, queries) + (keys,) * NF + (values,) * NF + (cols, rows, core_grad)
    saved_specs = [whole(blocks, SPAN, SPAN)] + [whole(blocks, *state)] * 3
    params = pltpu.CompilerParams(vmem_limit_bytes=48 << 20)
    per_stretch = jax.ShapeDtypeStruct((heads, blocks) + state, F32)
    per_head = jax.ShapeDtypeStruct((heads,) + state, F32)
    *saved, total_map, total_offset, total_pull = pl.pallas_call(
        functools.partial(maps_kernel, INVERSE_PASSES),
        grid=(heads,),
        in_specs=common_specs,
        out_specs=saved_specs + [whole(*state)] * 3,
        out_shape=[jax.ShapeDtypeStruct((heads, blocks, SPAN, SPAN), F32)]
        + [per_stretch] * 3
        + [per_head] * 3,
        compiler_params=params,
        name="local_maps",
    )(*common)
    enter, leave = chain(total_map, total_offset, total_pull)
    lanes = jax.ShapeDtypeStruct((length, heads * width), BF16)
    core_rows, dq, dk0, dk1, dk2, dv0, dv1, dv2, col_out, row_out = pl.pallas_call(
        functools.partial(results_kernel, RESULT_PASSES),
        grid=(heads,),
        in_specs=common_specs + saved_specs + [whole(*state)] * 2,
        out_specs=[lane_block(0)] * (2 + 2 * NF) + [whole(length, 8), whole(8, length)],
        out_shape=[lanes] * (2 + 2 * NF)
        + [
            jax.ShapeDtypeStruct((heads, length, 8), F32),
            jax.ShapeDtypeStruct((heads, 8, length), F32),
        ],
        compiler_params=params,
        name="results",
    )(*common, *saved, enter, leave)

    partial_out = jnp.dot(core_rows, out_weight, preferred_element_type=F32)
    mixed = lax.psum_scatter(partial_out, "head", scatter_dimension=1, tiled=True).astype(BF16)
    portion = lax.psum_scatter(
        jnp.einsum("td,te->de", cot_rows, core_rows, preferred_element_type=F32),
        "ctx",
        scatter_dimension=0,
        tiled=True,
    )
    weight_grad = lax.psum(portion, "dp")
    cumul_grad = (col_out[:, :, 3] + row_out[:, 0, :]).reshape(heads, blocks, CH)
    decay_grad = jnp.dot(cumul_grad, ordered.T, precision=high).reshape(heads, length)
    gate_grad = -decay_rate[:, None] * jax.nn.sigmoid(gate_logit[0]) * decay_grad
    rate_grad = lax.psum(-jnp.sum(soft * decay_grad, axis=1), ("ctx", "dp"))
    beta_grad = col_out[:, :, :NF].transpose(0, 2, 1) * (2.0 * sigmoid * (1.0 - sigmoid))

    def factors(pieces):
        return jnp.stack([p.reshape(length, heads, width) for p in pieces], axis=1)[None]

    return (
        mixed[None],
        dq.reshape(query_input.shape),
        factors((dk0, dk1, dk2)),
        factors((dv0, dv1, dv2)),
        beta_grad[None],
        gate_grad[None],
        weight_grad,
        rate_grad,
    )


INVERSE_PASSES = 3
RESULT_PASSES = 3


def solution(mesh):
    in_specs = (
        P(("groups", "dp"), "ctx", "head", None),
        P(("groups", "dp"), "ctx", None, "head", None),
        P(("groups", "dp"), "ctx", None, "head", None),
        P(("groups", "dp"), "head", None, "ctx"),
        P(("groups", "dp"), "head", "ctx"),
        P("head"),
        P(("groups", "dp"), None),
        P("head", None),
        P(("groups", "dp"), "ctx", None),
    )
    out_specs = (
        P(("groups", "dp"), "ctx", "head"),
        P(("groups", "dp"), "ctx", "head", None),
        P(("groups", "dp"), "ctx", None, "head", None),
        P(("groups", "dp"), "ctx", None, "head", None),
        P(("groups", "dp"), "head", None, "ctx"),
        P(("groups", "dp"), "head", "ctx"),
        P(("groups", "ctx"), "head"),
        P(("groups", "head")),
    )
    return jax.shard_map(
        on_device, mesh=mesh, in_specs=in_specs, out_specs=out_specs, check_vma=False
    )
```

```python
import functools

import jax
import jax.numpy as jnp
from jax import lax
from jax.experimental import pallas as pl
from jax.experimental.pallas import tpu as pltpu
from jax.sharding import PartitionSpec as P

CH = 64
NF = 3
SPAN = CH * NF
F32 = jnp.float32
BF16 = jnp.bfloat16


def mm(a, b, ta=False, tb=False, passes=1):
    dims = (((0 if ta else 1,), (1 if tb else 0,)), ((), ()))

    def one(x, y):
        return lax.dot_general(x, y, dims, preferred_element_type=F32)

    a_high, b_high = a.astype(BF16), b.astype(BF16)
    result = one(a_high, b_high)
    if passes == 3:
        a_low = (a - a_high.astype(F32)).astype(BF16)
        b_low = (b - b_high.astype(F32)).astype(BF16)
        result = result + one(a_high, b_low) + one(a_low, b_high)
    return result


def order_masks():
    row = lax.broadcasted_iota(jnp.int32, (SPAN, SPAN), 0)
    column = lax.broadcasted_iota(jnp.int32, (SPAN, SPAN), 1)
    row_time = (row % CH) * NF + row // CH
    column_time = (column % CH) * NF + column // CH
    return row_time > column_time, row_time ^ column_time


def load_stretch(s, q_ref, k_refs, v_refs, cols_ref, rows_ref):
    at = slice(s * CH, (s + 1) * CH)
    q = q_ref[at, :].astype(F32) * (q_ref.shape[-1] ** (-0.5))
    raw = jnp.concatenate([ref[at, :] for ref in k_refs], axis=0).astype(F32)
    v = jnp.concatenate([ref[at, :] for ref in v_refs], axis=0).astype(F32)
    inverse_norm = lax.rsqrt(jnp.sum(raw * raw, axis=1, keepdims=True) + 1e-06)
    k = raw * inverse_norm
    cols = cols_ref[0, at, :]
    beta = jnp.concatenate([cols[:, f : f + 1] for f in range(NF)], axis=0)
    token_cumul = cols[:, 3:4]
    token_last = cols[CH - 1 : CH, 3:4]
    cumul_row = rows_ref[0, 0:1, at]
    i = lax.broadcasted_iota(jnp.int32, (CH, CH), 0)
    j = lax.broadcasted_iota(jnp.int32, (CH, CH), 1)
    decay = jnp.where(i >= j, jnp.exp(jnp.where(i >= j, token_cumul - cumul_row, 0.0)), 0.0)
    read_decay = jnp.concatenate([decay] * NF, axis=1)
    growth = jnp.exp(token_cumul)
    tail = jnp.exp(token_last - token_cumul)
    return dict(
        q=q,
        k=k,
        v=v,
        inverse_norm=inverse_norm,
        beta=beta,
        read_decay=read_decay,
        pair_decay=jnp.concatenate([read_decay] * NF, axis=0),
        read_growth=growth,
        growth=jnp.concatenate([growth] * NF, axis=0),
        tail=jnp.concatenate([tail] * NF, axis=0),
        last=jnp.exp(token_last),
    )


def maps_kernel(
    passes, retain_ref, q_ref, k0, k1, k2, v0, v1, v2, cols_ref, rows_ref, grad_ref,
    inverse_ref, map_ref, offset_ref, pull_ref, total_map_ref, total_offset_ref, total_pull_ref,
):
    strict, differing = order_masks()
    width = q_ref.shape[-1]
    count = q_ref.shape[0] // CH
    diagonal = (
        lax.broadcasted_iota(jnp.int32, (width, width), 0)
        == lax.broadcasted_iota(jnp.int32, (width, width), 1)
    )
    parts = [load_stretch(s, q_ref, (k0, k1, k2), (v0, v1, v2), cols_ref, rows_ref) for s in range(count)]
    lowers, inverses = [], []
    for part in parts:
        gram = mm(part["k"], part["k"], tb=True, passes=passes)
        lower = jnp.where(strict, part["beta"] * part["pair_decay"] * gram, 0.0)
        lowers.append(lower)
        inverses.append(
            jnp.where(differing == 0, 1.0, 0.0) - jnp.where(differing == 1, lower, 0.0)
        )
    for level in range(1, (SPAN - 1).bit_length()):
        here = (differing >> level) == 1
        halves = [mm(jnp.where(here, low, 0.0), inv, passes=passes) for low, inv in zip(lowers, inverses)]
        inverses = [inv - mm(inv, half, passes=passes) for inv, half in zip(inverses, halves)]
    maps, offsets, pulls = [], [], []
    for s, (part, inverse) in enumerate(zip(parts, inverses)):
        inverse_ref[0, s] = inverse
        right = part["beta"] * jnp.concatenate([part["v"], part["growth"] * part["k"]], axis=1)
        solved = mm(inverse, right, passes=passes)
        moved = mm(part["tail"] * part["k"], solved, ta=True, passes=passes)
        offsets.append(moved[:, :width])
        maps.append(jnp.where(diagonal, part["last"], 0.0) - moved[:, width:])
        reads = mm(part["q"], part["k"], tb=True, passes=passes) * part["read_decay"]
        route = part["read_growth"] * part["q"] - mm(reads, solved[:, width:], passes=passes)
        pulls.append(mm(route, grad_ref[s * CH : (s + 1) * CH, :], ta=True, passes=passes))
        map_ref[0, s] = maps[-1]
        offset_ref[0, s] = offsets[-1]
        pull_ref[0, s] = pulls[-1]
    total_map, total_offset = retain_ref[0] * maps[0], offsets[0]
    for s in range(1, count):
        kept = retain_ref[s] * maps[s]
        total_map = mm(kept, total_map, passes=3)
        total_offset = mm(kept, total_offset, passes=3) + offsets[s]
    total_pull = retain_ref[count - 1] * pulls[-1]
    for s in range(count - 2, -1, -1):
        total_pull = retain_ref[s] * (pulls[s] + mm(maps[s], total_pull, ta=True, passes=3))
    total_map_ref[0] = total_map
    total_offset_ref[0] = total_offset
    total_pull_ref[0] = total_pull


def results_kernel(
    passes, retain_ref, q_ref, k0, k1, k2, v0, v1, v2, cols_ref, rows_ref, grad_ref,
    inverse_ref, map_ref, offset_ref, pull_ref, enter_ref, leave_ref,
    core_ref, dq_ref, dk0, dk1, dk2, dv0, dv1, dv2, col_out_ref, row_out_ref,
):
    strict, _ = order_masks()
    width = q_ref.shape[-1]
    count = q_ref.shape[0] // CH
    entries = [retain_ref[0] * enter_ref[0]]
    for s in range(1, count):
        entries.append(
            retain_ref[s] * (mm(map_ref[0, s - 1], entries[-1], passes=passes) + offset_ref[0, s - 1])
        )
    exits = [leave_ref[0]]
    for s in range(count - 1, 0, -1):
        exits.insert(
            0, retain_ref[s] * (mm(map_ref[0, s], exits[0], ta=True, passes=passes) + pull_ref[0, s])
        )
    mul = functools.partial(mm, passes=passes)
    for s in range(count):
        at = slice(s * CH, (s + 1) * CH)
        part = load_stretch(s, q_ref, (k0, k1, k2), (v0, v1, v2), cols_ref, rows_ref)
        q, k, beta, growth, tail = part["q"], part["k"], part["beta"], part["growth"], part["tail"]
        entry, leaving, grad = entries[s], exits[s], grad_ref[at, :]
        inverse = inverse_ref[0, s]
        gram = mul(k, k, tb=True)
        pair_decay = jnp.where(strict, part["pair_decay"], 0.0)
        on_entry = mul(jnp.concatenate([k, q], axis=0), entry)
        key_entry, query_entry = on_entry[:SPAN], on_entry[SPAN:]
        rest = part["v"] - growth * key_entry
        correction = mul(inverse, beta * rest)
        reads = mul(q, k, tb=True) * part["read_decay"]
        core_ref[at, :] = (part["read_growth"] * query_entry + mul(reads, correction)).astype(BF16)
        correction_grad = mul(reads, grad, ta=True) + tail * mul(k, leaving)
        right_grad = mul(inverse, correction_grad, ta=True)
        rest_grad = beta * right_grad
        outer = mul(jnp.concatenate([right_grad, grad], axis=0), correction, tb=True)
        scaled = -outer[:SPAN] * pair_decay
        reads_grad = outer[SPAN:]
        paired = scaled * gram
        paired_rows = jnp.sum(paired, axis=1, keepdims=True)
        beta_grad = jnp.sum(right_grad * rest, axis=1, keepdims=True) + paired_rows
        gram_grad = beta * scaled
        score_grad = reads_grad * part["read_decay"]
        read_pairs = reads_grad * reads
        back = mul(
            jnp.concatenate([-growth * rest_grad, part["read_growth"] * grad], axis=0), entry, tb=True
        )
        tail_grad = tail * mul(correction, leaving, tb=True)
        direct = mul(jnp.concatenate([gram_grad, score_grad], axis=0), k)
        query_grad = back[SPAN:] + direct[SPAN:]
        key_grad = (
            back[:SPAN] + direct[:SPAN] + tail_grad
            + mul(jnp.concatenate([gram_grad, score_grad], axis=0), jnp.concatenate([k, q], axis=0), ta=True)
        )
        tail_sums = jnp.sum(tail_grad * k, axis=1, keepdims=True)
        factor_cumul = (
            beta * paired_rows
            - growth * jnp.sum(rest_grad * key_entry, axis=1, keepdims=True)
            - tail_sums
        )
        token_cumul = (
            jnp.sum(read_pairs, axis=1, keepdims=True)
            + part["read_growth"] * jnp.sum(grad * query_entry, axis=1, keepdims=True)
        )
        for f in range(NF):
            token_cumul = token_cumul + factor_cumul[f * CH : (f + 1) * CH]
        last_grad = jnp.sum(tail_sums, axis=0, keepdims=True) + part["last"] * jnp.sum(
            jnp.sum(entry * leaving, axis=1, keepdims=True), axis=0, keepdims=True
        )
        token = lax.broadcasted_iota(jnp.int32, (CH, 1), 0)
        token_cumul = token_cumul + jnp.where(token == CH - 1, last_grad, 0.0)
        columns = jnp.sum(beta * paired, axis=0, keepdims=True) + jnp.sum(
            read_pairs, axis=0, keepdims=True
        )
        column_sums = columns[:, :CH]
        for f in range(1, NF):
            column_sums = column_sums + columns[:, f * CH : (f + 1) * CH]
        key_grad = part["inverse_norm"] * (
            key_grad - k * jnp.sum(k * key_grad, axis=1, keepdims=True)
        )
        dq_ref[at, :] = (query_grad * (width ** (-0.5))).astype(BF16)
        for f, (dk_ref, dv_ref) in enumerate(((dk0, dv0), (dk1, dv1), (dk2, dv2))):
            dk_ref[at, :] = key_grad[f * CH : (f + 1) * CH].astype(BF16)
            dv_ref[at, :] = rest_grad[f * CH : (f + 1) * CH].astype(BF16)
        col_out_ref[0, at, :] = jnp.concatenate(
            [beta_grad[f * CH : (f + 1) * CH] for f in range(NF)]
            + [token_cumul, jnp.zeros((CH, 4), F32)],
            axis=1,
        )
        row_out_ref[0, :, at] = jnp.broadcast_to(-column_sums, (8, CH))


def widen_kernel(narrow_ref, wide_ref):
    wide_ref[...] = narrow_ref[...].astype(F32)


def shifted(value, axis, steps):
    count = lax.axis_size(axis)
    first, last = (max(0, -steps), min(count, count - steps))
    return lax.ppermute(value, axis, [(source, source + steps) for source in range(first, last)])


def cyclic(value, axis, steps):
    count = lax.axis_size(axis)
    if steps == 0:
        return value
    moved = lax.ppermute(
        lax.optimization_barrier(value), axis, [(i, (i + steps) % count) for i in range(count)]
    )
    return lax.optimization_barrier(moved)


def column_slab(value, step, axis):
    count = lax.axis_size(axis)
    size = value.shape[1] // count
    owner = lax.rem(lax.axis_index(axis) + step, count)
    return lax.dynamic_slice_in_dim(value, owner * size, size, 1)


def scattered_sum(value, axis):
    return sum(
        cyclic(column_slab(value, step, axis), axis, step) for step in range(lax.axis_size(axis))
    )


def exchanged_sum(value, axis):
    if lax.axis_size(axis) == 2:
        return value + cyclic(value, axis, 1)
    return lax.psum(value, axis)


def chain(total_map, total_offset, total_pull):
    turns = lax.axis_size("ctx") - 1
    high = lax.Precision.HIGHEST
    enter = jnp.zeros_like(total_offset)
    leave = jnp.zeros_like(total_pull)
    for _ in range(turns):
        enter = shifted(
            jnp.einsum("swa,sag->swg", total_map, enter, precision=high) + total_offset, "ctx", 1
        )
        leave = shifted(
            jnp.einsum("saw,sag->swg", total_map, leave, precision=high) + total_pull, "ctx", -1
        )
    return enter, leave


def on_device(
    query_input, key_input, value_input, beta_logit, gate_logit, decay_rate,
    doc_ids, out_weight, out_cotangent,
):
    high = lax.Precision.HIGHEST
    _, length, heads, width = query_input.shape
    model_width = out_cotangent.shape[-1]
    blocks = length // CH
    padded = jnp.concatenate([jnp.full((1, 1), -1, jnp.int32), doc_ids], axis=1)
    window = lax.dynamic_slice_in_dim(padded, lax.axis_index("ctx") * blocks, blocks + 1, 1)
    retain = (window[0, 1:] == window[0, :-1]).astype(F32)

    queries = query_input.reshape(length, heads * width)
    keys = key_input.reshape(length, NF * heads * width)
    values = value_input.reshape(length, NF * heads * width)
    sigmoid = jax.nn.sigmoid(beta_logit[0])
    betas = 2.0 * sigmoid
    soft = jax.nn.softplus(gate_logit[0])
    log_decay = (-decay_rate[:, None] * soft).reshape(heads, blocks, CH)
    ordered = (jnp.arange(CH)[:, None] <= jnp.arange(CH)[None, :]).astype(F32)
    cumulative = jnp.dot(log_decay, ordered, precision=high).reshape(heads, 1, length)
    rows = jnp.broadcast_to(cumulative, (heads, 8, length))
    cols = jnp.concatenate(
        [betas, cumulative, jnp.zeros((heads, 4, length), F32)], axis=1
    ).transpose(0, 2, 1)

    cot_rows = out_cotangent.reshape(length, model_width)
    ctx_size = lax.axis_size("ctx")
    slab_width = model_width // ctx_size
    wide_rows = pl.pallas_call(
        widen_kernel, out_shape=jax.ShapeDtypeStruct(cot_rows.shape, F32), name="widen"
    )(cot_rows)
    slabs = [
        cyclic(column_slab(wide_rows, step, "ctx"), "ctx", step) for step in range(ctx_size)
    ]
    core_grad = lax.dot_general(
        cot_rows, out_weight, (((1,), (1,)), ((), ())), preferred_element_type=F32
    )

    def lane_block(f):
        return pl.BlockSpec((length, width), lambda h: (0, f * heads + h))

    def whole(*shape):
        return pl.BlockSpec((1,) + shape, lambda h: (h,) + (0,) * len(shape))

    state = (width, width)
    common_specs = (
        [pl.BlockSpec(memory_space=pltpu.SMEM), lane_block(0)]
        + [lane_block(f) for f in range(NF)] * 2
        + [whole(length, 8), whole(8, length), lane_block(0)]
    )
    common = (retain, queries) + (keys,) * NF + (values,) * NF + (cols, rows, core_grad)
    saved_specs = [whole(blocks, SPAN, SPAN)] + [whole(blocks, *state)] * 3
    params = pltpu.CompilerParams(vmem_limit_bytes=48 << 20)
    per_stretch = jax.ShapeDtypeStruct((heads, blocks) + state, F32)
    per_head = jax.ShapeDtypeStruct((heads,) + state, F32)
    *saved, total_map, total_offset, total_pull = pl.pallas_call(
        functools.partial(maps_kernel, INVERSE_PASSES),
        grid=(heads,),
        in_specs=common_specs,
        out_specs=saved_specs + [whole(*state)] * 3,
        out_shape=[jax.ShapeDtypeStruct((heads, blocks, SPAN, SPAN), F32)]
        + [per_stretch] * 3
        + [per_head] * 3,
        compiler_params=params,
        name="local_maps",
    )(*common)
    enter, leave = chain(total_map, total_offset, total_pull)
    lanes = jax.ShapeDtypeStruct((length, heads * width), BF16)
    core_rows, dq, dk0, dk1, dk2, dv0, dv1, dv2, col_out, row_out = pl.pallas_call(
        functools.partial(results_kernel, RESULT_PASSES),
        grid=(heads,),
        in_specs=common_specs + saved_specs + [whole(*state)] * 2,
        out_specs=[lane_block(0)] * (2 + 2 * NF) + [whole(length, 8), whole(8, length)],
        out_shape=[lanes] * (2 + 2 * NF)
        + [
            jax.ShapeDtypeStruct((heads, length, 8), F32),
            jax.ShapeDtypeStruct((heads, 8, length), F32),
        ],
        compiler_params=params,
        name="results",
    )(*common, *saved, enter, leave)

    cumul_grad = (col_out[:, :, 3] + row_out[:, 0, :]).reshape(heads, blocks, CH)
    decay_grad = jnp.dot(cumul_grad, ordered.T, precision=high).reshape(heads, length)
    gate_grad = -decay_rate[:, None] * jax.nn.sigmoid(gate_logit[0]) * decay_grad
    rate_part = jnp.pad(-jnp.sum(soft * decay_grad, axis=1), (0, (width - 1) * heads))
    sent = jnp.concatenate(
        [core_rows.astype(F32), jnp.broadcast_to(rate_part, (8, heads * width))], axis=0
    )
    gathered = lax.optimization_barrier(lax.all_gather(sent, "ctx", axis=0))
    sources = [lax.rem(lax.axis_index("ctx") - step + ctx_size, ctx_size) for step in range(ctx_size)]
    partial_weight = sum(
        lax.dot_general(
            slab,
            lax.dynamic_index_in_dim(gathered, source, 0, keepdims=False)[:length],
            (((0,), (0,)), ((), ())),
            precision=high,
            preferred_element_type=F32,
        )
        for slab, source in zip(slabs, sources)
    )
    totals = exchanged_sum(
        jnp.concatenate([partial_weight, jnp.sum(gathered[:, length:], axis=0)], axis=0), "dp"
    )
    weight_grad = totals[:slab_width]
    rate_grad = totals[slab_width, :heads]
    partial_out = jnp.dot(core_rows, out_weight, preferred_element_type=F32)
    mixed = scattered_sum(partial_out, "head").astype(BF16)
    beta_grad = col_out[:, :, :NF].transpose(0, 2, 1) * (2.0 * sigmoid * (1.0 - sigmoid))

    def factors(pieces):
        return jnp.stack([p.reshape(length, heads, width) for p in pieces], axis=1)[None]

    return (
        mixed[None],
        dq.reshape(query_input.shape),
        factors((dk0, dk1, dk2)),
        factors((dv0, dv1, dv2)),
        beta_grad[None],
        gate_grad[None],
        weight_grad,
        rate_grad,
    )


INVERSE_PASSES = 3
RESULT_PASSES = 3


def solution(mesh):
    in_specs = (
        P(("groups", "dp"), "ctx", "head", None),
        P(("groups", "dp"), "ctx", None, "head", None),
        P(("groups", "dp"), "ctx", None, "head", None),
        P(("groups", "dp"), "head", None, "ctx"),
        P(("groups", "dp"), "head", "ctx"),
        P("head"),
        P(("groups", "dp"), None),
        P("head", None),
        P(("groups", "dp"), "ctx", None),
    )
    out_specs = (
        P(("groups", "dp"), "ctx", "head"),
        P(("groups", "dp"), "ctx", "head", None),
        P(("groups", "dp"), "ctx", None, "head", None),
        P(("groups", "dp"), "ctx", None, "head", None),
        P(("groups", "dp"), "head", None, "ctx"),
        P(("groups", "dp"), "head", "ctx"),
        P(("groups", "ctx"), "head"),
        P(("groups", "head")),
    )
    return jax.shard_map(
        on_device, mesh=mesh, in_specs=in_specs, out_specs=out_specs, check_vma=False
    )
```

```python
import functools

import jax
import jax.numpy as jnp
from jax import lax
from jax.experimental import pallas as pl
from jax.experimental.pallas import tpu as pltpu
from jax.sharding import PartitionSpec as P

CH = 64
NF = 3
SPAN = CH * NF
F32 = jnp.float32
BF16 = jnp.bfloat16


def mm(a, b, ta=False, tb=False, passes=1):
    dims = (((0 if ta else 1,), (1 if tb else 0,)), ((), ()))

    def one(x, y):
        return lax.dot_general(x, y, dims, preferred_element_type=F32)

    a_high, b_high = a.astype(BF16), b.astype(BF16)
    result = one(a_high, b_high)
    if passes == 3:
        a_low = (a - a_high.astype(F32)).astype(BF16)
        b_low = (b - b_high.astype(F32)).astype(BF16)
        result = result + one(a_high, b_low) + one(a_low, b_high)
    return result


def order_masks():
    row = lax.broadcasted_iota(jnp.int32, (SPAN, SPAN), 0)
    column = lax.broadcasted_iota(jnp.int32, (SPAN, SPAN), 1)
    row_time = (row % CH) * NF + row // CH
    column_time = (column % CH) * NF + column // CH
    return row_time > column_time, row_time ^ column_time


def load_stretch(s, q_ref, k_refs, v_refs, cols_ref, rows_ref):
    at = slice(s * CH, (s + 1) * CH)
    q = q_ref[at, :].astype(F32) * (q_ref.shape[-1] ** (-0.5))
    raw = jnp.concatenate([ref[at, :] for ref in k_refs], axis=0).astype(F32)
    v = jnp.concatenate([ref[at, :] for ref in v_refs], axis=0).astype(F32)
    inverse_norm = lax.rsqrt(jnp.sum(raw * raw, axis=1, keepdims=True) + 1e-06)
    k = raw * inverse_norm
    cols = cols_ref[0, at, :]
    beta = jnp.concatenate([cols[:, f : f + 1] for f in range(NF)], axis=0)
    token_cumul = cols[:, 3:4]
    token_last = cols[CH - 1 : CH, 3:4]
    cumul_row = rows_ref[0, 0:1, at]
    i = lax.broadcasted_iota(jnp.int32, (CH, CH), 0)
    j = lax.broadcasted_iota(jnp.int32, (CH, CH), 1)
    decay = jnp.where(i >= j, jnp.exp(jnp.where(i >= j, token_cumul - cumul_row, 0.0)), 0.0)
    read_decay = jnp.concatenate([decay] * NF, axis=1)
    growth = jnp.exp(token_cumul)
    tail = jnp.exp(token_last - token_cumul)
    return dict(
        q=q,
        k=k,
        v=v,
        inverse_norm=inverse_norm,
        beta=beta,
        read_decay=read_decay,
        pair_decay=jnp.concatenate([read_decay] * NF, axis=0),
        read_growth=growth,
        growth=jnp.concatenate([growth] * NF, axis=0),
        tail=jnp.concatenate([tail] * NF, axis=0),
        last=jnp.exp(token_last),
    )


def maps_kernel(
    passes, retain_ref, q_ref, k0, k1, k2, v0, v1, v2, cols_ref, rows_ref, grad_ref,
    inverse_ref, map_ref, offset_ref, pull_ref, total_map_ref, total_offset_ref, total_pull_ref,
):
    strict, differing = order_masks()
    width = q_ref.shape[-1]
    count = q_ref.shape[0] // CH
    diagonal = (
        lax.broadcasted_iota(jnp.int32, (width, width), 0)
        == lax.broadcasted_iota(jnp.int32, (width, width), 1)
    )
    parts = [load_stretch(s, q_ref, (k0, k1, k2), (v0, v1, v2), cols_ref, rows_ref) for s in range(count)]
    lowers, inverses = [], []
    for part in parts:
        gram = mm(part["k"], part["k"], tb=True, passes=passes)
        lower = jnp.where(strict, part["beta"] * part["pair_decay"] * gram, 0.0)
        lowers.append(lower)
        inverses.append(
            jnp.where(differing == 0, 1.0, 0.0) - jnp.where(differing == 1, lower, 0.0)
        )
    for level in range(1, (SPAN - 1).bit_length()):
        here = (differing >> level) == 1
        halves = [mm(jnp.where(here, low, 0.0), inv, passes=passes) for low, inv in zip(lowers, inverses)]
        inverses = [inv - mm(inv, half, passes=passes) for inv, half in zip(inverses, halves)]
    maps, offsets, pulls = [], [], []
    for s, (part, inverse) in enumerate(zip(parts, inverses)):
        inverse_ref[0, s] = inverse
        right = part["beta"] * jnp.concatenate([part["v"], part["growth"] * part["k"]], axis=1)
        solved = mm(inverse, right, passes=passes)
        moved = mm(part["tail"] * part["k"], solved, ta=True, passes=passes)
        offsets.append(moved[:, :width])
        maps.append(jnp.where(diagonal, part["last"], 0.0) - moved[:, width:])
        reads = mm(part["q"], part["k"], tb=True, passes=passes) * part["read_decay"]
        route = part["read_growth"] * part["q"] - mm(reads, solved[:, width:], passes=passes)
        pulls.append(mm(route, grad_ref[s * CH : (s + 1) * CH, :], ta=True, passes=passes))
        map_ref[0, s] = maps[-1]
        offset_ref[0, s] = offsets[-1]
        pull_ref[0, s] = pulls[-1]
    total_map, total_offset = retain_ref[0] * maps[0], offsets[0]
    for s in range(1, count):
        kept = retain_ref[s] * maps[s]
        total_map = mm(kept, total_map, passes=3)
        total_offset = mm(kept, total_offset, passes=3) + offsets[s]
    total_pull = retain_ref[count - 1] * pulls[-1]
    for s in range(count - 2, -1, -1):
        total_pull = retain_ref[s] * (pulls[s] + mm(maps[s], total_pull, ta=True, passes=3))
    total_map_ref[0] = total_map
    total_offset_ref[0] = total_offset
    total_pull_ref[0] = total_pull


def results_kernel(
    passes, retain_ref, q_ref, k0, k1, k2, v0, v1, v2, cols_ref, rows_ref, grad_ref,
    inverse_ref, map_ref, offset_ref, pull_ref, enter_ref, leave_ref,
    core_ref, dq_ref, dk0, dk1, dk2, dv0, dv1, dv2, col_out_ref, row_out_ref,
):
    strict, _ = order_masks()
    width = q_ref.shape[-1]
    count = q_ref.shape[0] // CH
    entries = [retain_ref[0] * enter_ref[0]]
    for s in range(1, count):
        entries.append(
            retain_ref[s] * (mm(map_ref[0, s - 1], entries[-1], passes=passes) + offset_ref[0, s - 1])
        )
    exits = [leave_ref[0]]
    for s in range(count - 1, 0, -1):
        exits.insert(
            0, retain_ref[s] * (mm(map_ref[0, s], exits[0], ta=True, passes=passes) + pull_ref[0, s])
        )
    mul = functools.partial(mm, passes=passes)
    for s in range(count):
        at = slice(s * CH, (s + 1) * CH)
        part = load_stretch(s, q_ref, (k0, k1, k2), (v0, v1, v2), cols_ref, rows_ref)
        q, k, beta, growth, tail = part["q"], part["k"], part["beta"], part["growth"], part["tail"]
        entry, leaving, grad = entries[s], exits[s], grad_ref[at, :]
        inverse = inverse_ref[0, s]
        gram = mul(k, k, tb=True)
        pair_decay = jnp.where(strict, part["pair_decay"], 0.0)
        on_entry = mul(jnp.concatenate([k, q], axis=0), entry)
        key_entry, query_entry = on_entry[:SPAN], on_entry[SPAN:]
        rest = part["v"] - growth * key_entry
        correction = mul(inverse, beta * rest)
        reads = mul(q, k, tb=True) * part["read_decay"]
        core_ref[at, :] = (part["read_growth"] * query_entry + mul(reads, correction)).astype(BF16)
        correction_grad = mul(reads, grad, ta=True) + tail * mul(k, leaving)
        right_grad = mul(inverse, correction_grad, ta=True)
        rest_grad = beta * right_grad
        outer = mul(jnp.concatenate([right_grad, grad], axis=0), correction, tb=True)
        scaled = -outer[:SPAN] * pair_decay
        reads_grad = outer[SPAN:]
        paired = scaled * gram
        paired_rows = jnp.sum(paired, axis=1, keepdims=True)
        beta_grad = jnp.sum(right_grad * rest, axis=1, keepdims=True) + paired_rows
        gram_grad = beta * scaled
        score_grad = reads_grad * part["read_decay"]
        read_pairs = reads_grad * reads
        back = mul(
            jnp.concatenate([-growth * rest_grad, part["read_growth"] * grad], axis=0), entry, tb=True
        )
        tail_grad = tail * mul(correction, leaving, tb=True)
        direct = mul(jnp.concatenate([gram_grad, score_grad], axis=0), k)
        query_grad = back[SPAN:] + direct[SPAN:]
        key_grad = (
            back[:SPAN] + direct[:SPAN] + tail_grad
            + mul(jnp.concatenate([gram_grad, score_grad], axis=0), jnp.concatenate([k, q], axis=0), ta=True)
        )
        tail_sums = jnp.sum(tail_grad * k, axis=1, keepdims=True)
        factor_cumul = (
            beta * paired_rows
            - growth * jnp.sum(rest_grad * key_entry, axis=1, keepdims=True)
            - tail_sums
        )
        token_cumul = (
            jnp.sum(read_pairs, axis=1, keepdims=True)
            + part["read_growth"] * jnp.sum(grad * query_entry, axis=1, keepdims=True)
        )
        for f in range(NF):
            token_cumul = token_cumul + factor_cumul[f * CH : (f + 1) * CH]
        last_grad = jnp.sum(tail_sums, axis=0, keepdims=True) + part["last"] * jnp.sum(
            jnp.sum(entry * leaving, axis=1, keepdims=True), axis=0, keepdims=True
        )
        token = lax.broadcasted_iota(jnp.int32, (CH, 1), 0)
        token_cumul = token_cumul + jnp.where(token == CH - 1, last_grad, 0.0)
        columns = jnp.sum(beta * paired, axis=0, keepdims=True) + jnp.sum(
            read_pairs, axis=0, keepdims=True
        )
        column_sums = columns[:, :CH]
        for f in range(1, NF):
            column_sums = column_sums + columns[:, f * CH : (f + 1) * CH]
        key_grad = part["inverse_norm"] * (
            key_grad - k * jnp.sum(k * key_grad, axis=1, keepdims=True)
        )
        dq_ref[at, :] = (query_grad * (width ** (-0.5))).astype(BF16)
        for f, (dk_ref, dv_ref) in enumerate(((dk0, dv0), (dk1, dv1), (dk2, dv2))):
            dk_ref[at, :] = key_grad[f * CH : (f + 1) * CH].astype(BF16)
            dv_ref[at, :] = rest_grad[f * CH : (f + 1) * CH].astype(BF16)
        col_out_ref[0, at, :] = jnp.concatenate(
            [beta_grad[f * CH : (f + 1) * CH] for f in range(NF)]
            + [token_cumul, jnp.zeros((CH, 4), F32)],
            axis=1,
        )
        row_out_ref[0, :, at] = jnp.broadcast_to(-column_sums, (8, CH))


def widen_kernel(narrow_ref, wide_ref):
    wide_ref[...] = narrow_ref[...].astype(F32)


def shifted(value, axis, steps):
    count = lax.axis_size(axis)
    first, last = (max(0, -steps), min(count, count - steps))
    return lax.ppermute(value, axis, [(source, source + steps) for source in range(first, last)])


def cyclic(value, axis, steps):
    count = lax.axis_size(axis)
    if steps == 0:
        return value
    moved = lax.ppermute(
        lax.optimization_barrier(value), axis, [(i, (i + steps) % count) for i in range(count)]
    )
    return lax.optimization_barrier(moved)


def column_slab(value, step, axis):
    count = lax.axis_size(axis)
    size = value.shape[1] // count
    owner = lax.rem(lax.axis_index(axis) + step, count)
    return lax.dynamic_slice_in_dim(value, owner * size, size, 1)


def scattered_sum(value, axis):
    return sum(
        cyclic(column_slab(value, step, axis), axis, step) for step in range(lax.axis_size(axis))
    )


def exchanged_sum(value, axis):
    if lax.axis_size(axis) == 2:
        return value + cyclic(value, axis, 1)
    return lax.psum(value, axis)


def chain(total_map, total_offset, total_pull):
    turns = lax.axis_size("ctx") - 1
    high = lax.Precision.HIGHEST
    enter = jnp.zeros_like(total_offset)
    leave = jnp.zeros_like(total_pull)
    for _ in range(turns):
        enter = shifted(
            jnp.einsum("swa,sag->swg", total_map, enter, precision=high) + total_offset, "ctx", 1
        )
        leave = shifted(
            jnp.einsum("saw,sag->swg", total_map, leave, precision=high) + total_pull, "ctx", -1
        )
    return enter, leave


def on_device(
    query_input, key_input, value_input, beta_logit, gate_logit, decay_rate,
    doc_ids, out_weight, out_cotangent,
):
    high = lax.Precision.HIGHEST
    _, length, heads, width = query_input.shape
    model_width = out_cotangent.shape[-1]
    blocks = length // CH
    padded = jnp.concatenate([jnp.full((1, 1), -1, jnp.int32), doc_ids], axis=1)
    window = lax.dynamic_slice_in_dim(padded, lax.axis_index("ctx") * blocks, blocks + 1, 1)
    retain = (window[0, 1:] == window[0, :-1]).astype(F32)

    queries = query_input.reshape(length, heads * width)
    keys = key_input.reshape(length, NF * heads * width)
    values = value_input.reshape(length, NF * heads * width)
    sigmoid = jax.nn.sigmoid(beta_logit[0])
    betas = 2.0 * sigmoid
    soft = jax.nn.softplus(gate_logit[0])
    log_decay = (-decay_rate[:, None] * soft).reshape(heads, blocks, CH)
    ordered = (jnp.arange(CH)[:, None] <= jnp.arange(CH)[None, :]).astype(F32)
    cumulative = jnp.dot(log_decay, ordered, precision=high).reshape(heads, 1, length)
    rows = jnp.broadcast_to(cumulative, (heads, 8, length))
    cols = jnp.concatenate(
        [betas, cumulative, jnp.zeros((heads, 4, length), F32)], axis=1
    ).transpose(0, 2, 1)

    cot_rows = out_cotangent.reshape(length, model_width)
    ctx_size = lax.axis_size("ctx")
    slab_width = model_width // ctx_size
    wide_rows = pl.pallas_call(
        widen_kernel, out_shape=jax.ShapeDtypeStruct(cot_rows.shape, F32), name="widen"
    )(cot_rows)
    slabs = [
        cyclic(column_slab(wide_rows, step, "ctx"), "ctx", step) for step in range(ctx_size)
    ]
    core_grad = lax.dot_general(
        cot_rows, out_weight, (((1,), (1,)), ((), ())), preferred_element_type=F32
    )

    def lane_block(f):
        return pl.BlockSpec((length, width), lambda h: (0, f * heads + h))

    def whole(*shape):
        return pl.BlockSpec((1,) + shape, lambda h: (h,) + (0,) * len(shape))

    state = (width, width)
    common_specs = (
        [pl.BlockSpec(memory_space=pltpu.SMEM), lane_block(0)]
        + [lane_block(f) for f in range(NF)] * 2
        + [whole(length, 8), whole(8, length), lane_block(0)]
    )
    common = (retain, queries) + (keys,) * NF + (values,) * NF + (cols, rows, core_grad)
    saved_specs = [whole(blocks, SPAN, SPAN)] + [whole(blocks, *state)] * 3
    params = pltpu.CompilerParams(vmem_limit_bytes=48 << 20)
    per_stretch = jax.ShapeDtypeStruct((heads, blocks) + state, F32)
    per_head = jax.ShapeDtypeStruct((heads,) + state, F32)
    *saved, total_map, total_offset, total_pull = pl.pallas_call(
        functools.partial(maps_kernel, INVERSE_PASSES),
        grid=(heads,),
        in_specs=common_specs,
        out_specs=saved_specs + [whole(*state)] * 3,
        out_shape=[jax.ShapeDtypeStruct((heads, blocks, SPAN, SPAN), F32)]
        + [per_stretch] * 3
        + [per_head] * 3,
        compiler_params=params,
        cost_estimate=pl.CostEstimate(
            flops=6000 * heads * blocks * SPAN**3 // 64, bytes_accessed=16 << 20, transcendentals=0
        ),
        name="local_maps",
    )(*common)
    total_map, slabs = lax.optimization_barrier((total_map, slabs))
    enter, leave = chain(total_map, total_offset, total_pull)
    lanes = jax.ShapeDtypeStruct((length, heads * width), BF16)
    core_rows, dq, dk0, dk1, dk2, dv0, dv1, dv2, col_out, row_out = pl.pallas_call(
        functools.partial(results_kernel, RESULT_PASSES),
        grid=(heads,),
        in_specs=common_specs + saved_specs + [whole(*state)] * 2,
        out_specs=[lane_block(0)] * (2 + 2 * NF) + [whole(length, 8), whole(8, length)],
        out_shape=[lanes] * (2 + 2 * NF)
        + [
            jax.ShapeDtypeStruct((heads, length, 8), F32),
            jax.ShapeDtypeStruct((heads, 8, length), F32),
        ],
        compiler_params=params,
        name="results",
    )(*common, *saved, enter, leave)

    cumul_grad = (col_out[:, :, 3] + row_out[:, 0, :]).reshape(heads, blocks, CH)
    decay_grad = jnp.dot(cumul_grad, ordered.T, precision=high).reshape(heads, length)
    gate_grad = -decay_rate[:, None] * jax.nn.sigmoid(gate_logit[0]) * decay_grad
    rate_part = jnp.pad(-jnp.sum(soft * decay_grad, axis=1), (0, (width - 1) * heads))
    sent = jnp.concatenate(
        [core_rows.astype(F32), jnp.broadcast_to(rate_part, (8, heads * width))], axis=0
    )
    gathered = lax.optimization_barrier(lax.all_gather(sent, "ctx", axis=0))
    sources = [lax.rem(lax.axis_index("ctx") - step + ctx_size, ctx_size) for step in range(ctx_size)]
    partial_weight = sum(
        lax.dot_general(
            slab,
            lax.dynamic_index_in_dim(gathered, source, 0, keepdims=False)[:length],
            (((0,), (0,)), ((), ())),
            precision=high,
            preferred_element_type=F32,
        )
        for slab, source in zip(slabs, sources)
    )
    totals = exchanged_sum(
        jnp.concatenate([partial_weight, jnp.sum(gathered[:, length:], axis=0)], axis=0), "dp"
    )
    weight_grad = totals[:slab_width]
    rate_grad = totals[slab_width, :heads]
    partial_out = jnp.dot(core_rows, out_weight, preferred_element_type=F32)
    mixed = scattered_sum(partial_out, "head").astype(BF16)
    beta_grad = col_out[:, :, :NF].transpose(0, 2, 1) * (2.0 * sigmoid * (1.0 - sigmoid))

    def factors(pieces):
        return jnp.stack([p.reshape(length, heads, width) for p in pieces], axis=1)[None]

    return (
        mixed[None],
        dq.reshape(query_input.shape),
        factors((dk0, dk1, dk2)),
        factors((dv0, dv1, dv2)),
        beta_grad[None],
        gate_grad[None],
        weight_grad,
        rate_grad,
    )


INVERSE_PASSES = 3
RESULT_PASSES = 3


def solution(mesh):
    in_specs = (
        P(("groups", "dp"), "ctx", "head", None),
        P(("groups", "dp"), "ctx", None, "head", None),
        P(("groups", "dp"), "ctx", None, "head", None),
        P(("groups", "dp"), "head", None, "ctx"),
        P(("groups", "dp"), "head", "ctx"),
        P("head"),
        P(("groups", "dp"), None),
        P("head", None),
        P(("groups", "dp"), "ctx", None),
    )
    out_specs = (
        P(("groups", "dp"), "ctx", "head"),
        P(("groups", "dp"), "ctx", "head", None),
        P(("groups", "dp"), "ctx", None, "head", None),
        P(("groups", "dp"), "ctx", None, "head", None),
        P(("groups", "dp"), "head", None, "ctx"),
        P(("groups", "dp"), "head", "ctx"),
        P(("groups", "ctx"), "head"),
        P(("groups", "head")),
    )
    return jax.shard_map(
        on_device, mesh=mesh, in_specs=in_specs, out_specs=out_specs, check_vma=False
    )
```
